32 devices in a mesh: tm: 8 (over z, y), grid: 4 (over x, core).
Axes of the slice: x: 2, y: 2, z: 4, core: 2. Of those that a mesh axis runs over, the one named last changes fastest.
Arguments:
- departure: float32 [16, 64, 3, 1024], P('tm', 'grid'), may hold values from -6 to 6
- obs_weight: float32 [16, 64], P('tm', 'grid'), may hold values from 0.2 to 2
- obs_block: int32 [16, 64], P('tm', 'grid'), may hold values from 0 to 7
- coarse_decay: float32 [3, 32, 1024], P(None, 'grid'), may hold values from 0.95 to 1
Outputs:
- adjoint: float32 [16, 3, 32, 1024], P('tm', None, 'grid')
- misfit: float32 [], replicated
- changes: float32 [3], replicated
The draws below stay inside these ranges and needn't reach their ends.
Inputs may be any that keep to these rules, and one draw needn't show every extreme that they name: `obs_block`: several observations may name the same block.
All inputs are finite; a program needn't handle non-finite values.
Results may differ from the reference program's by a relative error of at most 0.0003.
Values sent between devices are 32-bit elements; how exact they have to be, the bound alone decides.
A program may use at most 64 MiB of HBM per device.

```python
import math
import jax
import jax.numpy as jnp
from jax import lax

ROWS_DEV = 8
NLON = 1024
OBS_DEV = 16
STEPS = 4
ITERS = 3
TILE_ROWS = 8
TILE_COLS = 128
SUBWINDOWS = 16
NLAT = 32
OBS = 64
TILE = 1024
BLOCKS_DEV = 8
N_GRID = 4


def plant(drawn, stream_key, low, largest):
    shape = drawn.shape
    index_at = [jax.random.randint(jax.random.fold_in(stream_key, axis), (), 0, shape[axis]) for axis in range(len(shape))]
    drawn = drawn.at[tuple(index_at)].set(low)
    longest = shape.index(max(shape))
    index_at[longest] = (index_at[longest] + 1) % shape[longest]
    return drawn.at[tuple(index_at)].set(largest)


def steps_of(stream_key, dims, split, smallest, largest):
    def one(axis_at, blocks):
        steps = jax.random.uniform(jax.random.fold_in(jax.random.fold_in(stream_key, 6), axis_at), (blocks,), jnp.float32, smallest / len(split), largest / len(split))
        return jnp.repeat(jnp.exp(steps), dims[axis_at] // blocks).reshape((-1,) + (1,) * (len(dims) - axis_at - 1))

    loudness = one(*split[0])
    for cut in split[1:]:
        loudness = loudness * one(*cut)
    return loudness


def noise(rng, dims, scale, reach, cuts=(), kind=jnp.bfloat16):
    entries = jax.random.normal(rng, dims, jnp.float32) * scale
    if len(cuts) > 0:
        entries = steps_of(rng, dims, cuts, -0.22, 0.18) * entries
    return jnp.clip(entries, min=-reach, max=reach).astype(kind)


def setup_inputs(seed: int = 0) -> dict:
    key_of = jax.random.split(jax.random.key(seed), 5)
    return {
        "departure": noise(key_of[0], (SUBWINDOWS, OBS, 3, TILE), 1.0, 6.0, ((0, 8), (1, 4)), jnp.float32),
        "obs_weight": jnp.clip(jnp.exp(math.log(2.0) - 2.3025851 * jax.random.uniform(key_of[1], (SUBWINDOWS, OBS), jnp.float32) ** steps_of(key_of[1], (SUBWINDOWS, OBS), ((0, 8), (1, 4)), -0.2, 0.2)), 0.2, 2.0),
        "obs_block": plant(jax.random.randint(key_of[2], (SUBWINDOWS, OBS), 0, BLOCKS_DEV), jax.random.fold_in(key_of[2], 1), 0, BLOCKS_DEV - 1).astype(jnp.int32),
        "coarse_decay": jnp.clip(0.95 + 0.050000012 * jax.random.uniform(key_of[3], (3, NLAT, NLON), jnp.float32) ** steps_of(key_of[3], (3, NLAT, NLON), ((1, 4),), -0.2, 0.2), 0.95, 1.0),
    }


wave_coef = 0.6
diffusion = 0.05
coriolis = 0.1
epsilon = 1e-6


def along_lon(values):
    return 0.5 * (jnp.roll(values, -1, -1) - jnp.roll(values, 1, -1))


def pad_rows(values):
    return jnp.pad(values, ((0, 0), (1, 1), (0, 0)))


def along_lat(values):
    padded = pad_rows(values)
    return 0.5 * (padded[:, 2:] - padded[:, :-2])


def laplace(values):
    padded = pad_rows(values)
    return padded[:, 2:] + padded[:, :-2] + jnp.roll(values, -1, -1) + jnp.roll(values, 1, -1) - 4.0 * values


def sweep_once(fields, inside):
    height, zonal, merid = fields[:, 0], fields[:, 1], fields[:, 2]
    weight = inside[None, :, None]
    height_new = (height + wave_coef * (along_lon(zonal) + along_lat(merid)) + diffusion * laplace(height)) * weight
    zonal_new = (zonal + wave_coef * along_lon(height_new) + coriolis * merid + diffusion * laplace(zonal)) * weight
    merid_new = (merid + wave_coef * along_lat(height_new) - coriolis * zonal + diffusion * laplace(merid)) * weight
    return jnp.stack([height_new, zonal_new, merid_new], axis=1)


def spread_tiles(scaled, blocks, row_count, lon_count):
    tile_rows_n = row_count // TILE_ROWS
    tile_cols_n = lon_count // TILE_COLS
    choose = (blocks[..., None] == jnp.arange(tile_rows_n * tile_cols_n, dtype=jnp.int32)).astype(jnp.float32)
    tiles = jnp.einsum("sob,soct->sbct", choose, scaled, precision=lax.Precision.HIGHEST)
    leading = scaled.shape[0]
    tiles = tiles.reshape(leading, tile_rows_n, tile_cols_n, 3, TILE_ROWS, TILE_COLS).transpose(0, 3, 1, 4, 2, 5)
    return tiles.reshape(leading, 3, row_count, lon_count)


def reference(departure, obs_weight, obs_block, coarse_decay):
    count = SUBWINDOWS
    emphasis = 1.0 + 2.0 * jnp.arange(count, dtype=jnp.float32) / (count - 1)
    misfit = 0.5 * jnp.sum(emphasis[:, None] * obs_weight * jnp.sum(departure * departure, axis=(2, 3)))
    scaled = departure * (emphasis[:, None] * obs_weight)[:, :, None, None]
    scaled = scaled.reshape(count * N_GRID, OBS_DEV, 3, TILE)
    blocks = obs_block.reshape(count * N_GRID, OBS_DEV)
    forcing = spread_tiles(scaled, blocks, ROWS_DEV, NLON)
    forcing = forcing.reshape(count, N_GRID, 3, ROWS_DEV, NLON).transpose(0, 2, 1, 3, 4).reshape(count, 3, NLAT, NLON)
    inside = jnp.ones((NLAT,), jnp.float32)

    def fine(fields):
        for repeat in range(STEPS):
            fields = sweep_once(fields, inside)
        return fields

    def backward(correction):
        def advance(carry, term):
            value = coarse_decay * carry + term
            return value, value
        start = jnp.zeros((3, NLAT, NLON), jnp.float32)
        return lax.scan(advance, start, correction, reverse=True)[1]

    adjoint = backward(forcing)
    changes = []
    for iteration in range(ITERS):
        above = jnp.concatenate([adjoint[1:], jnp.zeros_like(adjoint[:1])], axis=0)
        correction = fine(above) - coarse_decay * above + forcing
        renewed = backward(correction)
        weights = emphasis[:, None, None, None]
        change_sum = jnp.sum(weights * (renewed - adjoint) ** 2)
        size_sum = jnp.sum(weights * renewed ** 2)
        changes.append(change_sum / (size_sum + epsilon))
        adjoint = renewed
    return adjoint, misfit, jnp.stack(changes)
```

```python
import functools

import jax
import jax.numpy as jnp
from jax import lax
from jax.experimental import pallas as pl
from jax.experimental.pallas import tpu as pltpu
from jax.sharding import PartitionSpec as P

STEPS = 4
ITERS = 3
TILE_ROWS = 8
LANES = 128
CORES = 2
PAD = 32

wave_coef = 0.6
diffusion = 0.05
coriolis = 0.1
epsilon = 1e-06

MESH = pl.DeviceIdType.MESH
f32 = jnp.float32


def fine(p, q, r, row):
    rows = p.shape[0]

    def west_east(v):
        return pltpu.roll(v, 1, 1), pltpu.roll(v, LANES - 1, 1)

    def up_down(v):
        above = jnp.where(row == 0, 0.0, pltpu.roll(v, 1, 0))
        below = jnp.where(row == rows - 1, 0.0, pltpu.roll(v, rows - 1, 0))
        return above, below

    half = 0.5 * wave_coef
    keep = 1.0 - 4.0 * diffusion
    for _ in range(STEPS):
        pw, pe = west_east(p)
        pu, pd = up_down(p)
        qw, qe = west_east(q)
        qu, qd = up_down(q)
        rw, re = west_east(r)
        ru, rd = up_down(r)
        p = keep * p + half * ((qe - qw) + (rd - ru)) + diffusion * ((pw + pe) + (pu + pd))
        nw, ne = west_east(p)
        nu, nd = up_down(p)
        q, r = (
            keep * q + half * (ne - nw) + coriolis * r + diffusion * ((qw + qe) + (qu + qd)),
            keep * r + half * (nd - nu) - coriolis * q + diffusion * ((rw + re) + (ru + rd)),
        )
    return p, q, r


def kernel(T, G, dep, wt, blk, dec, adj, chg, mis, *scratch):
    (forc, win, recv, dwin, drecv, state, hold, delta, pack, ret, srow, sret, misv, misr) = scratch[:14]
    (snd, rcv, fsnd, frcv, dsnd, drcv, dfsnd, dfrcv, rsnd, rrcv, ssnd, srcv, msem) = scratch[14:]
    SD, OD, NF, TILE = dep.shape
    NLON = dec.shape[2]
    NB = NLON // LANES
    X = G // CORES
    NC = T * X
    S = NLON // NC
    R = LANES // S
    K = T * SD
    NI = SD * NF
    NV = pack.shape[1]
    rows = G * TILE_ROWS
    t = lax.axis_index("tm")
    g = lax.axis_index("grid")
    core = lax.rem(g, CORES)
    x = lax.div(g, CORES)
    c = t * X + x
    sibling = {"tm": t, "grid": x * CORES + (1 - core)}

    def peer(chip):
        return {"tm": lax.div(chip, X), "grid": lax.rem(chip, X) * CORES + core}

    def slot(chip):
        return lax.div(chip, X), lax.rem(chip, X) * CORES + core

    barrier = pltpu.get_barrier_semaphore()

    def greet(j, carry):
        pl.semaphore_signal(barrier, inc=1, device_id=peer(lax.rem(c + j, NC)), device_id_type=MESH)
        return carry

    lax.fori_loop(1, NC, greet, 0)
    pl.semaphore_signal(barrier, inc=1, device_id=sibling, device_id_type=MESH)

    sub = lax.broadcasted_iota(jnp.int32, (TILE_ROWS, LANES), 0)
    lane = lax.broadcasted_iota(jnp.int32, (TILE_ROWS, LANES), 1)
    cost = jnp.zeros((NF, NLON), f32)
    for s in range(SD):
        emph = 1.0 + 2.0 * (t * SD + s).astype(f32) / (K - 1)
        tiles = [[jnp.zeros((TILE_ROWS, LANES), f32) for _ in range(NB)] for _ in range(NF)]
        for o in range(OD):
            weight = emph * wt[s, o]
            choose = jnp.where(sub == blk[s, o], weight, 0.0)
            block = dep[s, o]
            cost = cost + (weight * block) * block
            for f in range(NF):
                for r in range(NB):
                    piece = dep[s, o, pl.ds(f, 1), pl.ds(r * LANES, LANES)]
                    tiles[f][r] = tiles[f][r] + choose * piece
        for f in range(NF):
            for r in range(NB):
                forc[pl.ds((s * NF + f) * NB * TILE_ROWS + r, NB, TILE_ROWS), :] = tiles[f][r]
    cost_row = jnp.sum(cost, axis=0, keepdims=True)
    total = cost_row[:, :LANES]
    for r in range(1, NB):
        total = total + cost_row[:, r * LANES : (r + 1) * LANES]
    misv[...] = total

    def window(read, chip):
        start = lax.rem(chip * S - PAD + NLON, NLON)
        b0 = lax.div(start, LANES)
        off = lax.rem(start, LANES)
        b1 = lax.rem(b0 + 1, NB)
        both = jnp.where(lane >= off, read(b0), read(b1))
        return pltpu.roll(both, lax.rem(LANES - off, LANES), 1)

    def cut(chip, carry):
        for i in range(NI):
            def read(b, i=i):
                at = pl.multiple_of((i * NB + b) * TILE_ROWS, TILE_ROWS)
                return forc[pl.ds(at, TILE_ROWS), :]
            win[chip, i] = window(read, chip)
        return carry

    lax.fori_loop(0, NC, cut, 0)
    for xx in range(X):
        for f in range(NF):
            def read(b, f=f):
                return dec[f, :, pl.ds(pl.multiple_of(b * LANES, LANES), LANES)]
            dwin[xx, f] = window(read, t * X + xx)

    pl.semaphore_wait(barrier, NC)

    def scatter(chip):
        return pltpu.make_async_remote_copy(
            src_ref=win.at[chip], dst_ref=recv.at[t, g], send_sem=snd.at[chip], recv_sem=rcv.at[c],
            device_id=peer(chip), device_id_type=MESH)

    def arrival(chip):
        tt, gg = slot(chip)
        return pltpu.make_async_remote_copy(
            src_ref=win.at[chip], dst_ref=recv.at[tt, gg], send_sem=snd.at[chip], recv_sem=rcv.at[chip],
            device_id=peer(chip), device_id_type=MESH)

    def forward(chip):
        tt, gg = slot(chip)
        return pltpu.make_async_remote_copy(
            src_ref=recv.at[tt, gg], dst_ref=recv.at[tt, gg], send_sem=fsnd.at[chip], recv_sem=frcv.at[chip],
            device_id=sibling, device_id_type=MESH)

    def from_sibling(chip):
        tt, gg = lax.div(chip, X), lax.rem(chip, X) * CORES + (1 - core)
        return pltpu.make_async_remote_copy(
            src_ref=recv.at[tt, gg], dst_ref=recv.at[tt, gg], send_sem=fsnd.at[chip], recv_sem=frcv.at[chip],
            device_id=sibling, device_id_type=MESH)

    def dscatter(xx):
        return pltpu.make_async_remote_copy(
            src_ref=dwin.at[xx], dst_ref=drecv.at[g], send_sem=dsnd.at[xx], recv_sem=drcv.at[x],
            device_id={"tm": t, "grid": xx * CORES + core}, device_id_type=MESH)

    def darrival(xx):
        return pltpu.make_async_remote_copy(
            src_ref=dwin.at[xx], dst_ref=drecv.at[xx * CORES + core], send_sem=dsnd.at[xx], recv_sem=drcv.at[xx],
            device_id={"tm": t, "grid": xx * CORES + core}, device_id_type=MESH)

    def dforward(xx):
        gg = xx * CORES + core
        return pltpu.make_async_remote_copy(
            src_ref=drecv.at[gg], dst_ref=drecv.at[gg], send_sem=dfsnd.at[xx], recv_sem=dfrcv.at[xx],
            device_id=sibling, device_id_type=MESH)

    def dfrom_sibling(xx):
        gg = xx * CORES + (1 - core)
        return pltpu.make_async_remote_copy(
            src_ref=drecv.at[gg], dst_ref=drecv.at[gg], send_sem=dfsnd.at[xx], recv_sem=dfrcv.at[xx],
            device_id=sibling, device_id_type=MESH)

    def send(j, carry):
        scatter(lax.rem(c + j, NC)).start()
        return carry

    lax.fori_loop(1, NC, send, 0)
    for j in range(1, X):
        dscatter(lax.rem(x + j, X)).start()
    cost_copy = pltpu.make_async_remote_copy(
        src_ref=misv, dst_ref=misr, send_sem=msem.at[0], recv_sem=msem.at[1],
        device_id=sibling, device_id_type=MESH)
    cost_copy.start()
    recv[t, g] = win[c]
    drecv[g] = dwin[x]
    forward(c).start()
    dforward(x).start()

    for j in range(1, X):
        xx = lax.rem(x - j + X, X)
        darrival(xx).wait_recv()
        dforward(xx).start()

    def pass_on(j, carry):
        chip = lax.rem(c - j + NC, NC)
        arrival(chip).wait_recv()
        forward(chip).start()
        return carry

    lax.fori_loop(1, NC, pass_on, 0)

    def take(chip, carry):
        from_sibling(chip).wait_recv()
        return carry

    lax.fori_loop(0, NC, take, 0)
    for xx in range(X):
        dfrom_sibling(xx).wait_recv()
    cost_copy.wait_recv()

    row = lax.broadcasted_iota(jnp.int32, (rows, LANES), 0)

    def decay(f):
        return drecv[:, f].reshape(rows, LANES)

    def forcing(tt, s, f):
        return recv[tt, :, s * NF + f].reshape(rows, LANES)

    def folded(values):
        out = None
        for v in values:
            square = v * v
            for b in range(G):
                part = square[b * TILE_ROWS : (b + 1) * TILE_ROWS]
                out = part if out is None else out + part
        return out

    zero = jnp.zeros((rows, LANES), f32)
    for f in range(NF):
        state[K, f] = zero

    def first_chain(i, carry):
        tt = T - 1 - i
        for s in reversed(range(SD)):
            k = tt * SD + s
            for f in range(NF):
                state[k, f] = decay(f) * state[k + 1, f] + forcing(tt, s, f)
        return carry

    lax.fori_loop(0, T, first_chain, 0)

    def body(i, carry):
        change, size = carry
        tt = T - 1 - i
        old = [hold[f] for f in range(NF)]
        e = [delta[f] for f in range(NF)]
        for s in reversed(range(SD)):
            k = tt * SD + s
            moved = fine(*old, row)
            here = [state[k, f] for f in range(NF)]
            new = [moved[f] + decay(f) * e[f] + forcing(tt, s, f) for f in range(NF)]
            e = [new[f] - here[f] for f in range(NF)]
            for f in range(NF):
                state[k, f] = new[f]
            emph = 1.0 + 2.0 * k.astype(f32) / (K - 1)
            change = change + emph * folded(e)
            size = size + emph * folded(new)
            old = here
        for f in range(NF):
            hold[f] = old[f]
            delta[f] = e[f]
        return change, size

    inside = (lane >= PAD) & (lane < PAD + S)
    flat = lax.broadcasted_iota(jnp.int32, (1, LANES), 1)
    sums = jnp.where(flat == 2 * ITERS, 0.5 * jnp.sum(misv[...] + misr[...]), 0.0)
    nothing = jnp.zeros((TILE_ROWS, LANES), f32)
    tail = nothing
    for n in range(ITERS):
        first = 1 if n + 1 >= SD and n > 0 else 0
        for f in range(NF):
            hold[f] = state[(T - first) * SD, f]
            delta[f] = zero
        if n == 0:
            change, tail = body(jnp.int32(0), (nothing, nothing))
            carry = lax.fori_loop(1, T, body, (change, tail))
        else:
            carry = lax.fori_loop(first, T, body, (nothing, tail if first else nothing))
        for at, value in ((n, carry[0]), (ITERS + n, carry[1])):
            sums = sums + jnp.where(flat == at, jnp.sum(jnp.where(inside, value, 0.0)), 0.0)
    srow[...] = sums

    place = lax.div(lane, S)
    q0 = lax.rem(c, R)

    def fill(chip, carry):
        tt, gg = slot(chip)
        for v in range(NV):
            packed = None
            for i in range(v * R, min((v + 1) * R, NI)):
                where = lax.rem(q0 + i, R)
                at = pl.multiple_of(gg * TILE_ROWS, TILE_ROWS)
                value = state[tt * SD + i // NF, i % NF, pl.ds(at, TILE_ROWS), :]
                turned = pltpu.roll(value, lax.rem(where * S - PAD + LANES, LANES), 1)
                packed = turned if packed is None else jnp.where(place == where, turned, packed)
            pack[chip, v] = packed
        return carry

    lax.fori_loop(0, NC, fill, 0)

    def give(chip):
        return pltpu.make_async_remote_copy(
            src_ref=pack.at[chip], dst_ref=ret.at[c], send_sem=rsnd.at[chip], recv_sem=rrcv.at[c],
            device_id=peer(chip), device_id_type=MESH)

    def got(chip):
        return pltpu.make_async_remote_copy(
            src_ref=pack.at[chip], dst_ref=ret.at[chip], send_sem=rsnd.at[chip], recv_sem=rrcv.at[chip],
            device_id=peer(chip), device_id_type=MESH)

    def tell(chip):
        return pltpu.make_async_remote_copy(
            src_ref=srow, dst_ref=sret.at[c], send_sem=ssnd.at[chip], recv_sem=srcv.at[c],
            device_id=peer(chip), device_id_type=MESH)

    def told(chip):
        return pltpu.make_async_remote_copy(
            src_ref=srow, dst_ref=sret.at[chip], send_sem=ssnd.at[chip], recv_sem=srcv.at[chip],
            device_id=peer(chip), device_id_type=MESH)

    def send_back(j, carry):
        chip = lax.rem(c + j, NC)
        tell(chip).start()
        give(chip).start()
        return carry

    lax.fori_loop(1, NC, send_back, 0)
    ret[c] = pack[c]
    sret[c] = srow[...]

    def sent(j, carry):
        chip = lax.rem(c + j, NC)
        scatter(chip).wait_send()
        forward(chip).wait_send()
        return carry

    lax.fori_loop(1, NC, sent, 0)
    forward(c).wait_send()
    for j in range(1, X):
        xx = lax.rem(x + j, X)
        dscatter(xx).wait_send()
        dforward(xx).wait_send()
    dforward(x).wait_send()
    cost_copy.wait_send()

    def receive(j, carry):
        chip = lax.rem(c - j + NC, NC)
        told(chip).wait_recv()
        got(chip).wait_recv()
        return carry

    lax.fori_loop(1, NC, receive, 0)

    for m in range(NB):
        for i in range(NI):
            value = ret[m * R, i // R]
            for q in range(1, R):
                value = jnp.where(place == (q + i) % R, ret[m * R + q, i // R], value)
            shift = (LANES - (i % R) * S) % LANES
            if shift:
                value = pltpu.roll(value, shift, 1)
            adj[i // NF, i % NF, :, m * LANES : (m + 1) * LANES] = value

    totals = sret[0]
    for m in range(1, NC):
        totals = totals + sret[m]
    ratio = totals / (pltpu.roll(totals, LANES - ITERS, 1) + epsilon)
    for n in range(ITERS):
        chg[n] = jnp.sum(jnp.where(flat == n, ratio, 0.0))
    mis[0] = jnp.sum(jnp.where(flat == 2 * ITERS, totals, 0.0))

    def done(j, carry):
        chip = lax.rem(c + j, NC)
        tell(chip).wait_send()
        give(chip).wait_send()
        return carry

    lax.fori_loop(1, NC, done, 0)


def solution(mesh, interpret=False):
    T, G = mesh.shape["tm"], mesh.shape["grid"]

    def per_device(departure, obs_weight, obs_block, coarse_decay):
        SD, OD, NF, TILE = departure.shape
        RD, NLON = coarse_decay.shape[1:]
        X = G // CORES
        NC = T * X
        S = NLON // NC
        R = LANES // S
        NI = SD * NF
        NV = -(-NI // R)
        K = T * SD
        NB = NLON // LANES
        assert RD == TILE_ROWS and TILE == TILE_ROWS * LANES and NB == TILE_ROWS
        assert S * R == LANES and S + 2 * PAD <= LANES and PAD >= 2 * STEPS * ITERS
        rows = G * TILE_ROWS
        vm = functools.partial(pltpu.VMEM, dtype=f32)
        tile = (TILE_ROWS, LANES)
        dma = pltpu.SemaphoreType.DMA
        adjoint, changes, misfit = pl.pallas_call(
            functools.partial(kernel, T, G),
            out_shape=(
                jax.ShapeDtypeStruct((SD, NF, RD, NLON), f32),
                jax.ShapeDtypeStruct((ITERS,), f32),
                jax.ShapeDtypeStruct((1,), f32),
            ),
            in_specs=[
                pl.BlockSpec(memory_space=pltpu.VMEM),
                pl.BlockSpec(memory_space=pltpu.SMEM),
                pl.BlockSpec(memory_space=pltpu.SMEM),
                pl.BlockSpec(memory_space=pltpu.VMEM),
            ],
            out_specs=(
                pl.BlockSpec(memory_space=pltpu.VMEM),
                pl.BlockSpec(memory_space=pltpu.SMEM),
                pl.BlockSpec(memory_space=pltpu.SMEM),
            ),
            scratch_shapes=[
                vm((NI * NB * TILE_ROWS, LANES)),
                vm((NC, NI) + tile),
                vm((T, G, NI) + tile),
                vm((X, NF) + tile),
                vm((G, NF) + tile),
                vm((K + 1, NF, rows, LANES)),
                vm((NF, rows, LANES)),
                vm((NF, rows, LANES)),
                vm((NC, NV) + tile),
                vm((NC, NV) + tile),
                vm((1, LANES)),
                vm((NC, 1, LANES)),
                vm((1, LANES)),
                vm((1, LANES)),
                dma((NC,)), dma((NC,)), dma((NC,)), dma((NC,)),
                dma((X,)), dma((X,)), dma((X,)), dma((X,)),
                dma((NC,)), dma((NC,)), dma((NC,)), dma((NC,)), dma((2,)),
            ],
            compiler_params=pltpu.CompilerParams(
                collective_id=0, has_side_effects=True, vmem_limit_bytes=60 * 1024 * 1024
            ),
        )(departure, obs_weight, obs_block, coarse_decay)
        return adjoint, misfit.reshape(()), changes

    return jax.shard_map(
        per_device,
        mesh=mesh,
        in_specs=(
            P("tm", "grid", None, None),
            P("tm", "grid"),
            P("tm", "grid"),
            P(None, "grid", None),
        ),
        out_specs=(P("tm", None, "grid", None), P(), P()),
        check_vma=False,
    )
```

```python
import functools

import jax
import jax.numpy as jnp
from jax import lax
from jax.experimental import pallas as pl
from jax.experimental.pallas import tpu as pltpu
from jax.sharding import PartitionSpec as P

STEPS = 4
ITERS = 3
TILE_ROWS = 8
LANES = 128
CORES = 2
PAD = 32

wave_coef = 0.6
diffusion = 0.05
coriolis = 0.1
epsilon = 1e-06

MESH = pl.DeviceIdType.MESH
f32 = jnp.float32


def fine(p, q, r, row):
    rows = p.shape[0]

    def west_east(v):
        return pltpu.roll(v, 1, 1), pltpu.roll(v, LANES - 1, 1)

    def up_down(v):
        above = jnp.where(row == 0, 0.0, pltpu.roll(v, 1, 0))
        below = jnp.where(row == rows - 1, 0.0, pltpu.roll(v, rows - 1, 0))
        return above, below

    half = 0.5 * wave_coef
    keep = 1.0 - 4.0 * diffusion
    for _ in range(STEPS):
        pw, pe = west_east(p)
        pu, pd = up_down(p)
        qw, qe = west_east(q)
        qu, qd = up_down(q)
        rw, re = west_east(r)
        ru, rd = up_down(r)
        p = keep * p + half * ((qe - qw) + (rd - ru)) + diffusion * ((pw + pe) + (pu + pd))
        nw, ne = west_east(p)
        nu, nd = up_down(p)
        q, r = (
            keep * q + half * (ne - nw) + coriolis * r + diffusion * ((qw + qe) + (qu + qd)),
            keep * r + half * (nd - nu) - coriolis * q + diffusion * ((rw + re) + (ru + rd)),
        )
    return p, q, r


def kernel(T, G, dep, wt, blk, dec, adj, chg, mis, *scratch):
    (forc, win, recv, dwin, drecv, state, hold, sums, pack, ret, srow, sret, misv, misr) = scratch[:14]
    (snd, rcv, fsnd, frcv, dsnd, drcv, dfsnd, dfrcv, rsnd, rrcv, ssnd, srcv, msem) = scratch[14:]
    SD, NF, OD, TILE = dep.shape
    NLON = dec.shape[2]
    NB = NLON // LANES
    X = G // CORES
    NC = T * X
    S = NLON // NC
    R = LANES // S
    K = T * SD
    NI = SD * NF
    NV = pack.shape[1]
    rows = G * TILE_ROWS
    t = lax.axis_index("tm")
    g = lax.axis_index("grid")
    core = lax.rem(g, CORES)
    x = lax.div(g, CORES)
    c = t * X + x
    sibling = {"tm": t, "grid": x * CORES + (1 - core)}

    def peer(chip):
        return {"tm": lax.div(chip, X), "grid": lax.rem(chip, X) * CORES + core}

    def slot(chip):
        return lax.div(chip, X), lax.rem(chip, X) * CORES + core

    barrier = pltpu.get_barrier_semaphore()

    def greet(j, carry):
        pl.semaphore_signal(barrier, inc=1, device_id=peer(lax.rem(c + j, NC)), device_id_type=MESH)
        return carry

    lax.fori_loop(1, NC, greet, 0)
    pl.semaphore_signal(barrier, inc=1, device_id=sibling, device_id_type=MESH)

    sub = lax.broadcasted_iota(jnp.int32, (TILE_ROWS, LANES), 0)
    lane = lax.broadcasted_iota(jnp.int32, (TILE_ROWS, LANES), 1)
    which = lax.broadcasted_iota(jnp.int32, (OD, LANES), 0)
    cost = jnp.zeros((OD, LANES), f32)
    for s in range(SD):
        emph = 1.0 + 2.0 * (t * SD + s).astype(f32) / (K - 1)
        tiles = [[jnp.zeros((TILE_ROWS, LANES), f32) for _ in range(NB)] for _ in range(NF)]
        weights = jnp.zeros((OD, LANES), f32)
        for o in range(OD):
            weight = emph * wt[s, o]
            weights = jnp.where(which == o, weight, weights)
            choose = jnp.where(sub == blk[s, o], weight, 0.0)
            for f in range(NF):
                for r in range(NB):
                    piece = dep[s, f, pl.ds(o, 1), pl.ds(r * LANES, LANES)]
                    tiles[f][r] = tiles[f][r] + choose * piece
        squares = jnp.zeros((OD, LANES), f32)
        for f in range(NF):
            for r in range(NB):
                piece = dep[s, f, :, pl.ds(r * LANES, LANES)]
                squares = squares + piece * piece
        cost = cost + weights * squares
        for f in range(NF):
            for r in range(NB):
                forc[pl.ds((s * NF + f) * NB * TILE_ROWS + r, NB, TILE_ROWS), :] = tiles[f][r]
    misv[...] = jnp.sum(cost, axis=0, keepdims=True)

    def window(read, chip):
        start = lax.rem(chip * S - PAD + NLON, NLON)
        b0 = lax.div(start, LANES)
        off = lax.rem(start, LANES)
        b1 = lax.rem(b0 + 1, NB)
        both = jnp.where(lane >= off, read(b0), read(b1))
        return pltpu.roll(both, lax.rem(LANES - off, LANES), 1)

    def cut(chip, carry):
        for i in range(NI):
            def read(b, i=i):
                at = pl.multiple_of((i * NB + b) * TILE_ROWS, TILE_ROWS)
                return forc[pl.ds(at, TILE_ROWS), :]
            win[chip, i] = window(read, chip)
        return carry

    lax.fori_loop(0, NC, cut, 0)
    for xx in range(X):
        for f in range(NF):
            def read(b, f=f):
                return dec[f, :, pl.ds(pl.multiple_of(b * LANES, LANES), LANES)]
            dwin[xx, f] = window(read, t * X + xx)

    pl.semaphore_wait(barrier, NC)

    def scatter(chip):
        return pltpu.make_async_remote_copy(
            src_ref=win.at[chip], dst_ref=recv.at[t, g], send_sem=snd.at[chip], recv_sem=rcv.at[c],
            device_id=peer(chip), device_id_type=MESH)

    def arrival(chip):
        tt, gg = slot(chip)
        return pltpu.make_async_remote_copy(
            src_ref=win.at[chip], dst_ref=recv.at[tt, gg], send_sem=snd.at[chip], recv_sem=rcv.at[chip],
            device_id=peer(chip), device_id_type=MESH)

    def forward(chip):
        tt, gg = slot(chip)
        return pltpu.make_async_remote_copy(
            src_ref=recv.at[tt, gg], dst_ref=recv.at[tt, gg], send_sem=fsnd.at[chip], recv_sem=frcv.at[chip],
            device_id=sibling, device_id_type=MESH)

    def from_sibling(chip):
        tt, gg = lax.div(chip, X), lax.rem(chip, X) * CORES + (1 - core)
        return pltpu.make_async_remote_copy(
            src_ref=recv.at[tt, gg], dst_ref=recv.at[tt, gg], send_sem=fsnd.at[chip], recv_sem=frcv.at[chip],
            device_id=sibling, device_id_type=MESH)

    def dscatter(xx):
        return pltpu.make_async_remote_copy(
            src_ref=dwin.at[xx], dst_ref=drecv.at[g], send_sem=dsnd.at[xx], recv_sem=drcv.at[x],
            device_id={"tm": t, "grid": xx * CORES + core}, device_id_type=MESH)

    def darrival(xx):
        return pltpu.make_async_remote_copy(
            src_ref=dwin.at[xx], dst_ref=drecv.at[xx * CORES + core], send_sem=dsnd.at[xx], recv_sem=drcv.at[xx],
            device_id={"tm": t, "grid": xx * CORES + core}, device_id_type=MESH)

    def dforward(xx):
        gg = xx * CORES + core
        return pltpu.make_async_remote_copy(
            src_ref=drecv.at[gg], dst_ref=drecv.at[gg], send_sem=dfsnd.at[xx], recv_sem=dfrcv.at[xx],
            device_id=sibling, device_id_type=MESH)

    def dfrom_sibling(xx):
        gg = xx * CORES + (1 - core)
        return pltpu.make_async_remote_copy(
            src_ref=drecv.at[gg], dst_ref=drecv.at[gg], send_sem=dfsnd.at[xx], recv_sem=dfrcv.at[xx],
            device_id=sibling, device_id_type=MESH)

    def send(j, carry):
        scatter(lax.rem(c + j, NC)).start()
        return carry

    lax.fori_loop(1, NC, send, 0)
    for j in range(1, X):
        dscatter(lax.rem(x + j, X)).start()
    cost_copy = pltpu.make_async_remote_copy(
        src_ref=misv, dst_ref=misr, send_sem=msem.at[0], recv_sem=msem.at[1],
        device_id=sibling, device_id_type=MESH)
    cost_copy.start()
    recv[t, g] = win[c]
    drecv[g] = dwin[x]
    forward(c).start()
    dforward(x).start()

    for j in range(1, X):
        xx = lax.rem(x - j + X, X)
        darrival(xx).wait_recv()
        dforward(xx).start()

    def relay(tt):
        for xx in range(X):
            chip = tt * X + xx

            @pl.when(chip != c)
            def _(chip=chip):
                arrival(chip).wait_recv()
                forward(chip).start()

    def take(tt):
        for xx in range(X):
            from_sibling(tt * X + xx).wait_recv()

    row = lax.broadcasted_iota(jnp.int32, (rows, LANES), 0)

    def decay(f):
        return drecv[:, f].reshape(rows, LANES)

    def forcing(tt, s, f):
        return recv[tt, :, s * NF + f].reshape(rows, LANES)

    def folded(values):
        out = None
        for v in values:
            square = v * v
            for b in range(G):
                part = square[b * TILE_ROWS : (b + 1) * TILE_ROWS]
                out = part if out is None else out + part
        return out

    def give(chip):
        return pltpu.make_async_remote_copy(
            src_ref=pack.at[chip], dst_ref=ret.at[c], send_sem=rsnd.at[chip], recv_sem=rrcv.at[c],
            device_id=peer(chip), device_id_type=MESH)

    def got(chip):
        return pltpu.make_async_remote_copy(
            src_ref=pack.at[chip], dst_ref=ret.at[chip], send_sem=rsnd.at[chip], recv_sem=rrcv.at[chip],
            device_id=peer(chip), device_id_type=MESH)

    def tell(chip):
        return pltpu.make_async_remote_copy(
            src_ref=srow, dst_ref=sret.at[c], send_sem=ssnd.at[chip], recv_sem=srcv.at[c],
            device_id=peer(chip), device_id_type=MESH)

    def told(chip):
        return pltpu.make_async_remote_copy(
            src_ref=srow, dst_ref=sret.at[chip], send_sem=ssnd.at[chip], recv_sem=srcv.at[chip],
            device_id=peer(chip), device_id_type=MESH)

    place = lax.div(lane, S)
    q0 = lax.rem(c, R)

    def send_back(tt):
        for xx in range(X):
            chip = tt * X + xx
            at = pl.multiple_of((xx * CORES + core) * TILE_ROWS, TILE_ROWS)
            for v in range(NV):
                packed = None
                for i in range(v * R, min((v + 1) * R, NI)):
                    where = lax.rem(q0 + i, R)
                    value = hold[i // NF, i % NF, pl.ds(at, TILE_ROWS), :]
                    turned = pltpu.roll(value, lax.rem(where * S - PAD + LANES, LANES), 1)
                    packed = turned if packed is None else jnp.where(place == where, turned, packed)
                pack[chip, v] = packed

            @pl.when(chip != c)
            def _(chip=chip):
                give(chip).start()

    def account(k, s, new):
        emph = 1.0 + 2.0 * k.astype(f32) / (K - 1)
        for n in range(ITERS):
            if k is not last:
                sums[n] = sums[n] + emph * folded([new[n + 1][f] - new[n][f] for f in range(NF)])
            sums[ITERS + n] = sums[ITERS + n] + emph * folded(new[n + 1])
        for n in range(ITERS + 1):
            for f in range(NF):
                state[n, f] = new[n][f]
        for f in range(NF):
            hold[s, f] = new[ITERS][f]

    last = jnp.int32(K - 1)
    relay(T - 1)
    if T > 1:
        relay(T - 2)
    take(T - 1)
    sums[...] = jnp.zeros(sums.shape, f32)
    account(last, SD - 1, [[forcing(T - 1, SD - 1, f) for f in range(NF)]] * (ITERS + 1))
    for xx in range(X):
        dfrom_sibling(xx).wait_recv()

    if SD == 1:
        send_back(T - 1)

    def step(i, carry):
        k = K - 2 - i
        tt = lax.div(k, SD)
        s = lax.rem(k, SD)

        @pl.when(s == SD - 1)
        def _():
            @pl.when(tt > 0)
            def _():
                relay(tt - 1)
            take(tt)

        old = [[state[n, f] for f in range(NF)] for n in range(ITERS + 1)]
        force = [recv[tt, :, s * NF + f].reshape(rows, LANES) for f in range(NF)]
        d = [decay(f) for f in range(NF)]
        new = [[d[f] * old[0][f] + force[f] for f in range(NF)]]
        for n in range(ITERS):
            moved = fine(*old[n], row)
            new.append([moved[f] + d[f] * (old[n + 1][f] - old[n][f]) + force[f] for f in range(NF)])
        account(k, s, new)

        @pl.when(s == 0)
        def _():
            send_back(tt)

        return carry

    lax.fori_loop(0, K - 1, step, 0)

    inside = (lane >= PAD) & (lane < PAD + S)
    flat = lax.broadcasted_iota(jnp.int32, (1, LANES), 1)
    cost_copy.wait_recv()
    line = jnp.where(flat == 2 * ITERS, 0.5 * jnp.sum(misv[...] + misr[...]), 0.0)
    for n in range(2 * ITERS):
        line = line + jnp.where(flat == n, jnp.sum(jnp.where(inside, sums[n], 0.0)), 0.0)
    srow[...] = line

    def tell_all(j, carry):
        tell(lax.rem(c + j, NC)).start()
        return carry

    lax.fori_loop(1, NC, tell_all, 0)
    ret[c] = pack[c]
    sret[c] = srow[...]

    def sent(j, carry):
        chip = lax.rem(c + j, NC)
        scatter(chip).wait_send()
        forward(chip).wait_send()
        return carry

    lax.fori_loop(1, NC, sent, 0)
    forward(c).wait_send()
    for j in range(1, X):
        xx = lax.rem(x + j, X)
        dscatter(xx).wait_send()
        dforward(xx).wait_send()
    dforward(x).wait_send()
    cost_copy.wait_send()

    def receive(j, carry):
        chip = lax.rem(c - j + NC, NC)
        told(chip).wait_recv()
        got(chip).wait_recv()
        return carry

    lax.fori_loop(1, NC, receive, 0)

    for m in range(NB):
        for i in range(NI):
            value = ret[m * R, i // R]
            for q in range(1, R):
                value = jnp.where(place == (q + i) % R, ret[m * R + q, i // R], value)
            shift = (LANES - (i % R) * S) % LANES
            if shift:
                value = pltpu.roll(value, shift, 1)
            adj[i // NF, i % NF, :, m * LANES : (m + 1) * LANES] = value

    totals = sret[0]
    for m in range(1, NC):
        totals = totals + sret[m]
    ratio = totals / (pltpu.roll(totals, LANES - ITERS, 1) + epsilon)
    for n in range(ITERS):
        chg[n] = jnp.sum(jnp.where(flat == n, ratio, 0.0))
    mis[0] = jnp.sum(jnp.where(flat == 2 * ITERS, totals, 0.0))

    def done(j, carry):
        chip = lax.rem(c + j, NC)
        tell(chip).wait_send()
        give(chip).wait_send()
        return carry

    lax.fori_loop(1, NC, done, 0)


def solution(mesh, interpret=False):
    T, G = mesh.shape["tm"], mesh.shape["grid"]

    def per_device(departure, obs_weight, obs_block, coarse_decay):
        SD, OD, NF, TILE = departure.shape
        RD, NLON = coarse_decay.shape[1:]
        X = G // CORES
        NC = T * X
        S = NLON // NC
        R = LANES // S
        NI = SD * NF
        NV = -(-NI // R)
        K = T * SD
        NB = NLON // LANES
        assert RD == TILE_ROWS and TILE == TILE_ROWS * LANES and NB == TILE_ROWS
        assert S * R == LANES and S + 2 * PAD <= LANES and PAD >= 2 * STEPS * ITERS
        rows = G * TILE_ROWS
        vm = functools.partial(pltpu.VMEM, dtype=f32)
        tile = (TILE_ROWS, LANES)
        dma = pltpu.SemaphoreType.DMA
        adjoint, changes, misfit = pl.pallas_call(
            functools.partial(kernel, T, G),
            out_shape=(
                jax.ShapeDtypeStruct((SD, NF, RD, NLON), f32),
                jax.ShapeDtypeStruct((ITERS,), f32),
                jax.ShapeDtypeStruct((1,), f32),
            ),
            in_specs=[
                pl.BlockSpec(memory_space=pltpu.VMEM),
                pl.BlockSpec(memory_space=pltpu.SMEM),
                pl.BlockSpec(memory_space=pltpu.SMEM),
                pl.BlockSpec(memory_space=pltpu.VMEM),
            ],
            out_specs=(
                pl.BlockSpec(memory_space=pltpu.VMEM),
                pl.BlockSpec(memory_space=pltpu.SMEM),
                pl.BlockSpec(memory_space=pltpu.SMEM),
            ),
            scratch_shapes=[
                vm((NI * NB * TILE_ROWS, LANES)),
                vm((NC, NI) + tile),
                vm((T, G, NI) + tile),
                vm((X, NF) + tile),
                vm((G, NF) + tile),
                vm((ITERS + 1, NF, rows, LANES)),
                vm((SD, NF, rows, LANES)),
                vm((2 * ITERS,) + tile),
                vm((NC, NV) + tile),
                vm((NC, NV) + tile),
                vm((1, LANES)),
                vm((NC, 1, LANES)),
                vm((1, LANES)),
                vm((1, LANES)),
                dma((NC,)), dma((NC,)), dma((NC,)), dma((NC,)),
                dma((X,)), dma((X,)), dma((X,)), dma((X,)),
                dma((NC,)), dma((NC,)), dma((NC,)), dma((NC,)), dma((2,)),
            ],
            compiler_params=pltpu.CompilerParams(
                collective_id=0, has_side_effects=True, vmem_limit_bytes=60 * 1024 * 1024
            ),
        )(departure.transpose(0, 2, 1, 3), obs_weight, obs_block, coarse_decay)
        return adjoint, misfit.reshape(()), changes

    return jax.shard_map(
        per_device,
        mesh=mesh,
        in_specs=(
            P("tm", "grid", None, None),
            P("tm", "grid"),
            P("tm", "grid"),
            P(None, "grid", None),
        ),
        out_specs=(P("tm", None, "grid", None), P(), P()),
        check_vma=False,
    )
```

```python
import functools

import jax
import jax.numpy as jnp
from jax import lax
from jax.experimental import pallas as pl
from jax.experimental.pallas import tpu as pltpu
from jax.sharding import PartitionSpec as P

STEPS = 4
ITERS = 3
TILE_ROWS = 8
LANES = 128
CORES = 2
PAD = 32

wave_coef = 0.6
diffusion = 0.05
coriolis = 0.1
epsilon = 1e-06

MESH = pl.DeviceIdType.MESH
f32 = jnp.float32


def fine(p, q, r, sub):
    count = p.shape[0] // TILE_ROWS

    def blocks(v):
        return [v[b * TILE_ROWS : (b + 1) * TILE_ROWS] for b in range(count)]

    def west_east(v):
        return [pltpu.roll(b, 1, 1) for b in v], [pltpu.roll(b, LANES - 1, 1) for b in v]

    def up_down(v):
        less = [jnp.zeros_like(v[0])] + [pltpu.roll(b, 1, 0) for b in v]
        more = [pltpu.roll(b, TILE_ROWS - 1, 0) for b in v] + [jnp.zeros_like(v[0])]
        above = [jnp.where(sub == 0, less[b], less[b + 1]) for b in range(count)]
        below = [jnp.where(sub == TILE_ROWS - 1, more[b + 1], more[b]) for b in range(count)]
        return above, below

    ratio = 0.5 * wave_coef / diffusion
    keep = 1.0 - 4.0 * diffusion
    every = range(count)
    p, q, r = [ratio * v for v in blocks(p)], blocks(q), blocks(r)
    pw, pe = west_east(p)
    pu, pd = up_down(p)
    for _ in range(STEPS):
        qw, qe = west_east(q)
        qu, qd = up_down(q)
        rw, re = west_east(r)
        ru, rd = up_down(r)
        p = [
            keep * p[b]
            + (0.5 * wave_coef * ratio) * ((qe[b] - qw[b]) + (rd[b] - ru[b]))
            + diffusion * ((pw[b] + pe[b]) + (pu[b] + pd[b]))
            for b in every
        ]
        pw, pe = west_east(p)
        pu, pd = up_down(p)
        turn = coriolis / diffusion
        q, r = (
            [
                keep * q[b]
                + diffusion * (((pe[b] - pw[b]) + turn * r[b]) + ((qw[b] + qe[b]) + (qu[b] + qd[b])))
                for b in every
            ],
            [
                keep * r[b]
                + diffusion * (((pd[b] - pu[b]) - turn * q[b]) + ((rw[b] + re[b]) + (ru[b] + rd[b])))
                for b in every
            ],
        )
    p = [(1.0 / ratio) * v for v in p]
    return [jnp.concatenate(v, axis=0) for v in (p, q, r)]


def kernel(T, G, dep_hbm, wt, blk, dec_hbm, ret, sret, *scratch):
    (forc, win, recv, dwin, drecv, state, hold, sums, pack, srow, misv, misr, dep, dec) = scratch[:14]
    (snd, rcv, fsnd, frcv, dsnd, drcv, dfsnd, dfrcv, rsnd, rrcv, ssnd, srcv, msem, isem) = scratch[14:]
    SD, NF, OD, TILE = dep.shape
    NLON = dec.shape[2]
    NB = NLON // LANES
    X = G // CORES
    NC = T * X
    S = NLON // NC
    R = LANES // S
    K = T * SD
    NI = SD * NF
    NV = pack.shape[1]
    rows = G * TILE_ROWS
    t = lax.axis_index("tm")
    g = lax.axis_index("grid")
    core = lax.rem(g, CORES)
    x = lax.div(g, CORES)
    c = t * X + x
    sibling = {"tm": t, "grid": x * CORES + (1 - core)}

    def peer(chip):
        return {"tm": lax.div(chip, X), "grid": lax.rem(chip, X) * CORES + core}

    def slot(chip):
        return lax.div(chip, X), lax.rem(chip, X) * CORES + core

    barrier = pltpu.get_barrier_semaphore()

    def greet(j, carry):
        pl.semaphore_signal(barrier, inc=1, device_id=peer(lax.rem(c + j, NC)), device_id_type=MESH)
        return carry

    lax.fori_loop(1, NC, greet, 0)
    pl.semaphore_signal(barrier, inc=1, device_id=sibling, device_id_type=MESH)

    dec_copy = pltpu.make_async_copy(dec_hbm, dec, isem.at[0])
    dep_copy = pltpu.make_async_copy(dep_hbm, dep, isem.at[1])
    dep_copy.start()
    dec_copy.start()
    dep_copy.wait()

    sub = lax.broadcasted_iota(jnp.int32, (TILE_ROWS, LANES), 0)
    lane = lax.broadcasted_iota(jnp.int32, (TILE_ROWS, LANES), 1)
    which = lax.broadcasted_iota(jnp.int32, (OD, LANES), 0)
    cost = jnp.zeros((OD, LANES), f32)
    for s in range(SD):
        emph = 1.0 + 2.0 * (t * SD + s).astype(f32) / (K - 1)
        tiles = [[jnp.zeros((TILE_ROWS, LANES), f32) for _ in range(NB)] for _ in range(NF)]
        weights = jnp.zeros((OD, LANES), f32)
        for o in range(OD):
            weight = emph * wt[s, o]
            weights = jnp.where(which == o, weight, weights)
            choose = jnp.where(sub == blk[s, o], weight, 0.0)
            for f in range(NF):
                for r in range(NB):
                    piece = dep[s, f, pl.ds(o, 1), pl.ds(r * LANES, LANES)]
                    tiles[f][r] = tiles[f][r] + choose * piece
        squares = jnp.zeros((OD, LANES), f32)
        for f in range(NF):
            for r in range(NB):
                piece = dep[s, f, :, pl.ds(r * LANES, LANES)]
                squares = squares + piece * piece
        cost = cost + weights * squares
        for f in range(NF):
            for r in range(NB):
                forc[pl.ds((s * NF + f) * NB * TILE_ROWS + r, NB, TILE_ROWS), :] = tiles[f][r]
    misv[...] = jnp.sum(cost, axis=0, keepdims=True)

    def window(read, chip):
        start = lax.rem(chip * S - PAD + NLON, NLON)
        b0 = lax.div(start, LANES)
        off = lax.rem(start, LANES)
        b1 = lax.rem(b0 + 1, NB)
        both = jnp.where(lane >= off, read(b0), read(b1))
        return pltpu.roll(both, lax.rem(LANES - off, LANES), 1)

    def cut(chip, carry):
        for i in range(NI):
            def read(b, i=i):
                at = pl.multiple_of((i * NB + b) * TILE_ROWS, TILE_ROWS)
                return forc[pl.ds(at, TILE_ROWS), :]
            win[chip, i] = window(read, chip)
        return carry

    lax.fori_loop(0, NC, cut, 0)
    dec_copy.wait()
    for xx in range(X):
        for f in range(NF):
            def read(b, f=f):
                return dec[f, :, pl.ds(pl.multiple_of(b * LANES, LANES), LANES)]
            dwin[xx, f] = window(read, t * X + xx)

    pl.semaphore_wait(barrier, NC)

    def scatter(chip):
        return pltpu.make_async_remote_copy(
            src_ref=win.at[chip], dst_ref=recv.at[t, g], send_sem=snd.at[chip], recv_sem=rcv.at[c],
            device_id=peer(chip), device_id_type=MESH)

    def arrival(chip):
        tt, gg = slot(chip)
        return pltpu.make_async_remote_copy(
            src_ref=win.at[chip], dst_ref=recv.at[tt, gg], send_sem=snd.at[chip], recv_sem=rcv.at[chip],
            device_id=peer(chip), device_id_type=MESH)

    def forward(chip):
        tt, gg = slot(chip)
        return pltpu.make_async_remote_copy(
            src_ref=recv.at[tt, gg], dst_ref=recv.at[tt, gg], send_sem=fsnd.at[chip], recv_sem=frcv.at[chip],
            device_id=sibling, device_id_type=MESH)

    def from_sibling(chip):
        tt, gg = lax.div(chip, X), lax.rem(chip, X) * CORES + (1 - core)
        return pltpu.make_async_remote_copy(
            src_ref=recv.at[tt, gg], dst_ref=recv.at[tt, gg], send_sem=fsnd.at[chip], recv_sem=frcv.at[chip],
            device_id=sibling, device_id_type=MESH)

    def dscatter(xx):
        return pltpu.make_async_remote_copy(
            src_ref=dwin.at[xx], dst_ref=drecv.at[g], send_sem=dsnd.at[xx], recv_sem=drcv.at[x],
            device_id={"tm": t, "grid": xx * CORES + core}, device_id_type=MESH)

    def darrival(xx):
        return pltpu.make_async_remote_copy(
            src_ref=dwin.at[xx], dst_ref=drecv.at[xx * CORES + core], send_sem=dsnd.at[xx], recv_sem=drcv.at[xx],
            device_id={"tm": t, "grid": xx * CORES + core}, device_id_type=MESH)

    def dforward(xx):
        gg = xx * CORES + core
        return pltpu.make_async_remote_copy(
            src_ref=drecv.at[gg], dst_ref=drecv.at[gg], send_sem=dfsnd.at[xx], recv_sem=dfrcv.at[xx],
            device_id=sibling, device_id_type=MESH)

    def dfrom_sibling(xx):
        gg = xx * CORES + (1 - core)
        return pltpu.make_async_remote_copy(
            src_ref=drecv.at[gg], dst_ref=drecv.at[gg], send_sem=dfsnd.at[xx], recv_sem=dfrcv.at[xx],
            device_id=sibling, device_id_type=MESH)

    def send(j, carry):
        chip = NC - 1 - j

        @pl.when(chip != c)
        def _():
            scatter(chip).start()
        return carry

    lax.fori_loop(0, NC, send, 0)
    for j in range(1, X):
        dscatter(lax.rem(x + j, X)).start()
    cost_copy = pltpu.make_async_remote_copy(
        src_ref=misv, dst_ref=misr, send_sem=msem.at[0], recv_sem=msem.at[1],
        device_id=sibling, device_id_type=MESH)
    cost_copy.start()
    recv[t, g] = win[c]
    drecv[g] = dwin[x]
    forward(c).start()
    dforward(x).start()

    for j in range(1, X):
        xx = lax.rem(x - j + X, X)
        darrival(xx).wait_recv()
        dforward(xx).start()

    def relay(tt):
        for xx in range(X):
            chip = tt * X + xx

            @pl.when(chip != c)
            def _(chip=chip):
                arrival(chip).wait_recv()
                forward(chip).start()

    def take(tt):
        for xx in range(X):
            from_sibling(tt * X + xx).wait_recv()


    def decay(f):
        return drecv[:, f].reshape(rows, LANES)

    def forcing(tt, s, f):
        return recv[tt, :, s * NF + f].reshape(rows, LANES)

    def folded(values):
        out = None
        for v in values:
            square = v * v
            for b in range(G):
                part = square[b * TILE_ROWS : (b + 1) * TILE_ROWS]
                out = part if out is None else out + part
        return out

    def give(chip):
        return pltpu.make_async_remote_copy(
            src_ref=pack.at[chip], dst_ref=ret.at[c], send_sem=rsnd.at[chip], recv_sem=rrcv.at[c],
            device_id=peer(chip), device_id_type=MESH)

    def got(chip):
        return pltpu.make_async_remote_copy(
            src_ref=pack.at[chip], dst_ref=ret.at[chip], send_sem=rsnd.at[chip], recv_sem=rrcv.at[chip],
            device_id=peer(chip), device_id_type=MESH)

    def tell(chip):
        return pltpu.make_async_remote_copy(
            src_ref=srow, dst_ref=sret.at[c], send_sem=ssnd.at[chip], recv_sem=srcv.at[c],
            device_id=peer(chip), device_id_type=MESH)

    def told(chip):
        return pltpu.make_async_remote_copy(
            src_ref=srow, dst_ref=sret.at[chip], send_sem=ssnd.at[chip], recv_sem=srcv.at[chip],
            device_id=peer(chip), device_id_type=MESH)

    place = lax.div(lane, S)
    q0 = lax.rem(c, R)

    def send_back(tt):
        for xx in range(X):
            chip = tt * X + xx
            at = pl.multiple_of((xx * CORES + core) * TILE_ROWS, TILE_ROWS)
            for v in range(NV):
                packed = None
                for i in range(v * R, min((v + 1) * R, NI)):
                    where = lax.rem(q0 + i, R)
                    value = hold[i // NF, i % NF, pl.ds(at, TILE_ROWS), :]
                    turned = pltpu.roll(value, lax.rem(where * S - PAD + LANES, LANES), 1)
                    packed = turned if packed is None else jnp.where(place == where, turned, packed)
                pack[chip, v] = packed

            @pl.when(chip != c)
            def _(chip=chip):
                give(chip).start()

    def account(k, s, new):
        emph = 1.0 + 2.0 * k.astype(f32) / (K - 1)
        for n in range(ITERS):
            if k is not last:
                sums[n] = sums[n] + emph * folded([new[n + 1][f] - new[n][f] for f in range(NF)])
            sums[ITERS + n] = sums[ITERS + n] + emph * folded(new[n + 1])
        for n in range(ITERS + 1):
            for f in range(NF):
                state[n, f] = new[n][f]
        for f in range(NF):
            hold[s, f] = new[ITERS][f]

    last = jnp.int32(K - 1)
    relay(T - 1)
    if T > 1:
        relay(T - 2)
    take(T - 1)
    sums[...] = jnp.zeros(sums.shape, f32)
    account(last, SD - 1, [[forcing(T - 1, SD - 1, f) for f in range(NF)]] * (ITERS + 1))
    for xx in range(X):
        dfrom_sibling(xx).wait_recv()

    if SD == 1:
        send_back(T - 1)

    def step(i, carry):
        k = K - 2 - i
        tt = lax.div(k, SD)
        s = lax.rem(k, SD)

        @pl.when(s == SD - 1)
        def _():
            @pl.when(tt > 0)
            def _():
                relay(tt - 1)
            take(tt)

        old = [[state[n, f] for f in range(NF)] for n in range(ITERS + 1)]
        force = [recv[tt, :, s * NF + f].reshape(rows, LANES) for f in range(NF)]
        d = [decay(f) for f in range(NF)]
        new = [[d[f] * old[0][f] + force[f] for f in range(NF)]]
        for n in range(ITERS):
            moved = fine(*old[n], sub)
            new.append([moved[f] + d[f] * (old[n + 1][f] - old[n][f]) + force[f] for f in range(NF)])
        account(k, s, new)

        @pl.when(s == 0)
        def _():
            send_back(tt)

        return carry

    lax.fori_loop(0, K - 1, step, 0)

    inside = (lane >= PAD) & (lane < PAD + S)
    flat = lax.broadcasted_iota(jnp.int32, (1, LANES), 1)
    cost_copy.wait_recv()
    line = jnp.where(flat == 2 * ITERS, 0.5 * jnp.sum(misv[...] + misr[...]), 0.0)
    for n in range(2 * ITERS):
        line = line + jnp.where(flat == n, jnp.sum(jnp.where(inside, sums[n], 0.0)), 0.0)
    srow[...] = line

    def tell_all(j, carry):
        tell(lax.rem(c + j, NC)).start()
        return carry

    lax.fori_loop(1, NC, tell_all, 0)
    ret[c] = pack[c]
    sret[c] = srow[...]

    def sent(j, carry):
        chip = lax.rem(c + j, NC)
        scatter(chip).wait_send()
        forward(chip).wait_send()
        return carry

    lax.fori_loop(1, NC, sent, 0)
    forward(c).wait_send()
    for j in range(1, X):
        xx = lax.rem(x + j, X)
        dscatter(xx).wait_send()
        dforward(xx).wait_send()
    dforward(x).wait_send()
    cost_copy.wait_send()

    def receive(j, carry):
        chip = lax.rem(c - j + NC, NC)
        told(chip).wait_recv()
        got(chip).wait_recv()
        return carry

    lax.fori_loop(1, NC, receive, 0)

    def done(j, carry):
        chip = lax.rem(c + j, NC)
        tell(chip).wait_send()
        give(chip).wait_send()
        return carry

    lax.fori_loop(1, NC, done, 0)


def finish(S, ret, sret, adj, chg, mis):
    SD, NF, RD, NLON = adj.shape
    NC = ret.shape[0]
    NI = SD * NF
    NB = NLON // LANES
    R = LANES // S
    place = lax.div(lax.broadcasted_iota(jnp.int32, (TILE_ROWS, LANES), 1), S)
    flat = lax.broadcasted_iota(jnp.int32, (1, LANES), 1)
    for m in range(NB):
        for i in range(NI):
            value = ret[m * R, i // R]
            for q in range(1, R):
                value = jnp.where(place == (q + i) % R, ret[m * R + q, i // R], value)
            shift = (LANES - (i % R) * S) % LANES
            if shift:
                value = pltpu.roll(value, shift, 1)
            adj[i // NF, i % NF, :, m * LANES : (m + 1) * LANES] = value

    totals = sret[0]
    for m in range(1, NC):
        totals = totals + sret[m]
    ratio = totals / (pltpu.roll(totals, LANES - ITERS, 1) + epsilon)
    for n in range(ITERS):
        chg[n] = jnp.sum(jnp.where(flat == n, ratio, 0.0))
    mis[0] = jnp.sum(jnp.where(flat == 2 * ITERS, totals, 0.0))


def solution(mesh, interpret=False):
    T, G = mesh.shape["tm"], mesh.shape["grid"]

    def per_device(departure, obs_weight, obs_block, coarse_decay):
        SD, OD, NF, TILE = departure.shape
        RD, NLON = coarse_decay.shape[1:]
        X = G // CORES
        NC = T * X
        S = NLON // NC
        R = LANES // S
        NI = SD * NF
        NV = -(-NI // R)
        K = T * SD
        NB = NLON // LANES
        assert RD == TILE_ROWS and TILE == TILE_ROWS * LANES and NB == TILE_ROWS
        assert S * R == LANES and S + 2 * PAD <= LANES and PAD >= 2 * STEPS * ITERS
        rows = G * TILE_ROWS
        vm = functools.partial(pltpu.VMEM, dtype=f32)
        tile = (TILE_ROWS, LANES)
        dma = pltpu.SemaphoreType.DMA
        back, lines = pl.pallas_call(
            functools.partial(kernel, T, G),
            out_shape=(
                jax.ShapeDtypeStruct((NC, NV) + tile, f32),
                jax.ShapeDtypeStruct((NC, 1, LANES), f32),
            ),
            in_specs=[
                pl.BlockSpec(memory_space=pltpu.HBM),
                pl.BlockSpec(memory_space=pltpu.SMEM),
                pl.BlockSpec(memory_space=pltpu.SMEM),
                pl.BlockSpec(memory_space=pltpu.HBM),
            ],
            out_specs=(
                pl.BlockSpec(memory_space=pltpu.VMEM),
                pl.BlockSpec(memory_space=pltpu.VMEM),
            ),
            scratch_shapes=[
                vm((NI * NB * TILE_ROWS, LANES)),
                vm((NC, NI) + tile),
                vm((T, G, NI) + tile),
                vm((X, NF) + tile),
                vm((G, NF) + tile),
                vm((ITERS + 1, NF, rows, LANES)),
                vm((SD, NF, rows, LANES)),
                vm((2 * ITERS,) + tile),
                vm((NC, NV) + tile),
                vm((1, LANES)),
                vm((1, LANES)),
                vm((1, LANES)),
                vm((SD, NF, OD, NLON)),
                vm((NF, RD, NLON)),
                dma((NC,)), dma((NC,)), dma((NC,)), dma((NC,)),
                dma((X,)), dma((X,)), dma((X,)), dma((X,)),
                dma((NC,)), dma((NC,)), dma((NC,)), dma((NC,)), dma((2,)), dma((2,)),
            ],
            compiler_params=pltpu.CompilerParams(
                collective_id=0, has_side_effects=True, vmem_limit_bytes=60 * 1024 * 1024
            ),
        )(departure.transpose(0, 2, 1, 3), obs_weight, obs_block, coarse_decay)
        adjoint, changes, misfit = pl.pallas_call(
            functools.partial(finish, S),
            out_shape=(
                jax.ShapeDtypeStruct((SD, NF, RD, NLON), f32),
                jax.ShapeDtypeStruct((ITERS,), f32),
                jax.ShapeDtypeStruct((1,), f32),
            ),
            in_specs=[pl.BlockSpec(memory_space=pltpu.VMEM)] * 2,
            out_specs=(
                pl.BlockSpec(memory_space=pltpu.VMEM),
                pl.BlockSpec(memory_space=pltpu.SMEM),
                pl.BlockSpec(memory_space=pltpu.SMEM),
            ),
            compiler_params=pltpu.CompilerParams(vmem_limit_bytes=60 * 1024 * 1024),
        )(back, lines)
        return adjoint, misfit.reshape(()), changes

    return jax.shard_map(
        per_device,
        mesh=mesh,
        in_specs=(
            P("tm", "grid", None, None),
            P("tm", "grid"),
            P("tm", "grid"),
            P(None, "grid", None),
        ),
        out_specs=(P("tm", None, "grid", None), P(), P()),
        check_vma=False,
    )
```
